32 devices in a mesh: dp: 4 (over y, x), seq: 4 (over z), feat: 2 (over core).
Axes of the slice: x: 2, y: 2, z: 4, core: 2. Of those that a mesh axis runs over, the one named last changes fastest.
Arguments:
- tokens: bfloat16 [16384, 2048], P(('dp', 'seq')), parts along dimension 0, may hold values from -6 to 6
- w_query: bfloat16 [2048, 256], P(None, 'feat'), may hold values from -0.125 to 0.125
- w_key: bfloat16 [2048, 256], P(None, 'feat'), may hold values from -0.125 to 0.125
- value_weight: bfloat16 [2048, 2048], P(None, 'feat'), may hold values from -0.125 to 0.125
- w_out: bfloat16 [2048, 2048], P(None, 'feat'), may hold values from -0.125 to 0.125
Outputs:
- mixed: bfloat16 [16384, 2048], P(('dp', 'seq'), 'feat'), parts along dimension 0
The draws below stay inside these ranges and needn't reach their ends.
There are 4 independent parts, one for each index of `dp`. The reference program is written for one: setup_inputs(seed, part) draws one part's arguments, and reference() takes and returns one part's arrays. A program takes and returns all parts, laid end to end along the dimension named above; an argument that names none is the same for every part. Nothing has to cross between parts.
All inputs are finite; a program needn't handle non-finite values.
Results may differ from the reference program's by a relative error of at most 0.009.
Values may be sent and summed in bfloat16 or wider, within the bound.
No kernel may reach another device: no remote copies, remote signals or barrier semaphores. Data moves between devices by JAX's collectives and lax.ppermute only.
A program may use at most 64 MiB of HBM per device.

```python
import jax
import jax.numpy as jnp
from jax import lax

D = 2048
H = 16
DK = 16
DV = 128
TOK_DEV = 1024
SEQUENCE_TOKENS = 4096
N_SEQ = 4


def block_scale(rng, dims, shards, smallest, high):
    def one(dim, shards_of):
        heights = jax.random.uniform(jax.random.fold_in(jax.random.fold_in(rng, 6), dim), (shards_of,), jnp.float32, smallest / len(shards), high / len(shards))
        return jnp.repeat(jnp.exp(heights), dims[dim] // shards_of).reshape((-1,) + (1,) * (len(dims) - dim - 1))

    factor_of = one(*shards[0])
    for cut in shards[1:]:
        factor_of = factor_of * one(*cut)
    return factor_of


def bell_draw(rng, extent, deviation, most, shards=(), dtype=jnp.bfloat16):
    drawn = deviation * jax.random.normal(rng, extent, jnp.float32)
    if shards:
        drawn = drawn * block_scale(rng, extent, shards, -0.22, 0.18)
    return jnp.clip(drawn, -most, most).astype(dtype)


def setup_inputs(seed: int = 0, part: int = 0) -> dict:
    keys = jax.random.split(jax.random.key(seed), 6)
    own_keys = jax.random.split(jax.random.fold_in(keys[5], part), 6)
    tokens = bell_draw(own_keys[0], (SEQUENCE_TOKENS, D), 1.0, 6.0, ((0, 4),))
    w_query = bell_draw(keys[1], (D, H * DK), D ** -0.5, 0.125, ((1, 2),))
    w_key = bell_draw(keys[2], (D, H * DK), D ** -0.5, 0.125, ((1, 2),))
    value_weight = bell_draw(keys[3], (D, H * DV), D ** -0.5, 0.125, ((1, 2),))
    w_out = bell_draw(keys[4], (H * DV, D), (H * DV) ** -0.5, 0.125, ((1, 2),))
    return dict(tokens=tokens, w_query=w_query, w_key=w_key, value_weight=value_weight, w_out=w_out)


def key_features(key_rows):
    as_float = key_rows.astype(jnp.float32)
    row_count = key_rows.shape[0]
    head_total = key_rows.shape[1]
    linear = jnp.transpose(as_float, (1, 2, 0))
    square = jnp.einsum('nha,nhb->habn', as_float, as_float).reshape(head_total, -1, row_count)
    ones_row = jnp.ones((head_total, 1, row_count), jnp.float32)
    return jnp.concatenate([ones_row, linear, square], axis=1).astype(jnp.bfloat16)

def query_features(query_rows):
    as_float = query_rows.astype(jnp.float32)
    row_count = query_rows.shape[0]
    head_total = query_rows.shape[1]
    linear = jnp.transpose(as_float, (1, 2, 0)) * 0.25
    square = jnp.einsum('nha,nhb->habn', as_float, as_float).reshape(head_total, -1, row_count) * (1.0 / 32.0)
    ones_row = jnp.ones((head_total, 1, row_count), jnp.float32)
    return jnp.concatenate([ones_row, linear, square], axis=1)

def block_numerator(query_rows, key_rows, value_matrix, earlier):
    query_float = query_rows.astype(jnp.float32)
    key_float = key_rows.astype(jnp.float32)
    value_single = value_matrix.astype(jnp.float32)
    row_count = query_rows.shape[0]
    scores = jnp.einsum('nha,mha->hnm', query_float, key_float) * 0.25
    causal = lax.broadcasted_iota(jnp.int32, (row_count, row_count), 0) >= lax.broadcasted_iota(jnp.int32, (row_count, row_count), 1)
    weight_tensors = jnp.where(causal[None], 1.0 + scores + 0.5 * scores * scores, 0.0).astype(jnp.bfloat16)
    local_portion = jnp.einsum('iot,tiw->oiw', weight_tensors.astype(jnp.float32), value_single)
    carried = jnp.einsum('hfn,hfd->nhd', query_features(query_rows), earlier, precision=lax.Precision.HIGHEST)
    block_state = jnp.einsum('hfn,nhd->hfd', key_features(key_rows).astype(jnp.float32), value_single)
    return (carried + local_portion, block_state)

def reference(tokens, w_query, w_key, value_weight, w_out):
    query_all = jnp.dot(tokens, w_query, preferred_element_type=jnp.float32).astype(jnp.bfloat16).reshape(N_SEQ, TOK_DEV, H, DK)
    key_all = jnp.dot(tokens, w_key, preferred_element_type=jnp.float32).astype(jnp.bfloat16).reshape(N_SEQ, TOK_DEV, H, DK)
    value_all = jnp.dot(tokens, value_weight, preferred_element_type=jnp.float32).astype(jnp.bfloat16).reshape(N_SEQ, TOK_DEV, H, DV)

    def advance(prefix, items):
        numerator, block_state = block_numerator(items[0], items[1], items[2], prefix)
        return (prefix + block_state, numerator)
    initial = jnp.zeros((H, 1 + DK + DK * DK, DV), jnp.float32)
    final_state, numerator = lax.scan(advance, initial, (query_all, key_all, value_all))
    scale = lax.rsqrt(lax.optimization_barrier(jnp.mean(numerator * numerator, axis=-1, keepdims=True)) + 1e-06)
    normalized_rows = (numerator * scale).reshape(N_SEQ * TOK_DEV, H * DV).astype(jnp.bfloat16)
    return jnp.dot(normalized_rows, w_out, preferred_element_type=jnp.float32).astype(jnp.bfloat16)
```

```python
import functools

import jax
import jax.numpy as jnp
from jax import lax
from jax.experimental import pallas as pl
from jax.experimental.pallas import tpu as pltpu
from jax.sharding import PartitionSpec as P

DK = 16
DV = 128
F32 = jnp.float32
BF16 = jnp.bfloat16


def feature_tiles(rows, linear, square, cross):
    half = DK // 2
    tiles = [rows * linear if linear != 1.0 else rows]
    for shift in range(half):
        other = rows if shift == 0 else pltpu.roll(rows, shift, 0)
        weight = square if shift == 0 else cross
        product = rows * other
        tiles.append(product * weight if weight != 1.0 else product)
    far = rows[:half] * rows[half:]
    one = (lax.broadcasted_iota(jnp.int32, far.shape, 0) == 0).astype(F32)
    tiles.append(jnp.concatenate([far * cross if cross != 1.0 else far, one], axis=0))
    return jnp.concatenate([tile.astype(BF16) for tile in tiles], axis=0)


def feature_count():
    return DK + (DK // 2) * DK + DK


def project_kernel(heads, x_ref, wq_ref, wk_ref, wv_ref, q_ref, kt_ref, v_ref, before_ref, total_ref, state):
    step = pl.program_id(0)

    @pl.when(step == 0)
    def _():
        state[...] = jnp.zeros_like(state)

    x = x_ref[...]
    width = heads * DK
    qk = jnp.dot(x, jnp.concatenate([wq_ref[...], wk_ref[...]], axis=1), preferred_element_type=F32)
    q_ref[...] = qk[:, :width].astype(BF16)
    kt = qk[:, width:].astype(BF16).astype(F32).T
    kt_ref[...] = kt.astype(BF16)
    before_ref[0] = state[...]
    for head in range(heads):
        cols = slice(head * DV, (head + 1) * DV)
        if head % 2 == 0:
            pair = slice(head * DV, (head + 2) * DV)
            v_ref[:, pair] = jnp.dot(x, wv_ref[:, pair], preferred_element_type=F32).astype(BF16)
        phi = feature_tiles(kt[head * DK : (head + 1) * DK], 1.0, 1.0, 1.0)
        state[head] += jnp.dot(phi, v_ref[:, cols], preferred_element_type=F32)
    total_ref[...] = state[...].astype(BF16)


def local_kernel(heads, q_ref, kt_ref, v_ref, num_ref, phi_ref):
    chunk = q_ref.shape[0]
    q = q_ref[...]
    kt = kt_ref[...]
    qf = q.astype(F32)
    qt = qf.T
    quarter = (qf * 0.25).astype(BF16)
    causal = lax.broadcasted_iota(jnp.int32, (chunk, chunk), 0) >= lax.broadcasted_iota(
        jnp.int32, (chunk, chunk), 1
    )
    owner = lax.broadcasted_iota(jnp.int32, kt.shape, 0) // DK
    for head in range(heads):
        keys = jnp.where(owner == head, kt, jnp.zeros_like(kt))
        s = jnp.dot(quarter, keys, preferred_element_type=F32)
        w = jnp.where(causal, 1.0 + s * (1.0 + 0.5 * s), 0.0).astype(BF16)
        cols = slice(head * DV, (head + 1) * DV)
        num_ref[:, cols] = jnp.dot(w, v_ref[:, cols], preferred_element_type=F32)
        phi = feature_tiles(qt[head * DK : (head + 1) * DK], 0.25, 1.0 / 32.0, 1.0 / 16.0)
        phi_ref[head] = phi.T


def carry_kernel(heads, num_ref, phi_ref, before_ref, prefix_ref, out_ref):
    for head in range(heads):
        cols = slice(head * DV, (head + 1) * DV)
        state = (before_ref[0, head] + prefix_ref[head].astype(F32)).astype(BF16)
        num = num_ref[:, cols] + jnp.dot(phi_ref[head], state, preferred_element_type=F32)
        scale = lax.rsqrt(jnp.mean(num * num, axis=-1, keepdims=True) + 1e-6)
        out_ref[:, cols] = (num * scale).astype(BF16)


def mix_kernel(order_ref, own_ref, other_ref, wown_ref, wother_ref, out_ref):
    total = jnp.dot(own_ref[...], wown_ref[...], preferred_element_type=F32)
    total += jnp.dot(other_ref[...], wother_ref[...], preferred_element_type=F32)
    out_ref[...] = total.astype(BF16)


def params(mib):
    return pltpu.CompilerParams(vmem_limit_bytes=mib << 20, dimension_semantics=("arbitrary",))


def project(x, w_query, w_key, value_weight, chunk):
    rows, depth = x.shape
    heads = value_weight.shape[1] // DV
    steps = rows // chunk
    count = feature_count()
    width = heads * DK
    return pl.pallas_call(
        functools.partial(project_kernel, heads),
        grid=(steps,),
        in_specs=[
            pl.BlockSpec((chunk, depth), lambda i: (i, 0)),
            pl.BlockSpec((depth, width), lambda i: (0, 0)),
            pl.BlockSpec((depth, width), lambda i: (0, 0)),
            pl.BlockSpec((depth, heads * DV), lambda i: (0, 0)),
        ],
        out_specs=[
            pl.BlockSpec((chunk, width), lambda i: (i, 0)),
            pl.BlockSpec((width, chunk), lambda i: (0, i)),
            pl.BlockSpec((chunk, heads * DV), lambda i: (i, 0)),
            pl.BlockSpec((1, heads, count, DV), lambda i: (i, 0, 0, 0)),
            pl.BlockSpec((heads, count, DV), lambda i: (0, 0, 0)),
        ],
        out_shape=[
            jax.ShapeDtypeStruct((rows, width), BF16),
            jax.ShapeDtypeStruct((width, rows), BF16),
            jax.ShapeDtypeStruct((rows, heads * DV), BF16),
            jax.ShapeDtypeStruct((steps, heads, count, DV), F32),
            jax.ShapeDtypeStruct((heads, count, DV), BF16),
        ],
        scratch_shapes=[pltpu.VMEM((heads, count, DV), F32)],
        compiler_params=params(32),
        cost_estimate=pl.CostEstimate(
            flops=2 * rows * depth * heads * (DV + 2 * DK), bytes_accessed=12 << 20, transcendentals=0
        ),
        name="project",
    )(x, w_query, w_key, value_weight)


def local_part(q, kt, v, chunk):
    rows, width = q.shape
    heads = width // DK
    count = feature_count()
    return pl.pallas_call(
        functools.partial(local_kernel, heads),
        grid=(rows // chunk,),
        in_specs=[
            pl.BlockSpec((chunk, width), lambda i: (i, 0)),
            pl.BlockSpec((width, chunk), lambda i: (0, i)),
            pl.BlockSpec((chunk, heads * DV), lambda i: (i, 0)),
        ],
        out_specs=[
            pl.BlockSpec((chunk, heads * DV), lambda i: (i, 0)),
            pl.BlockSpec((heads, chunk, count), lambda i: (0, i, 0)),
        ],
        out_shape=[
            jax.ShapeDtypeStruct((rows, heads * DV), F32),
            jax.ShapeDtypeStruct((heads, rows, count), BF16),
        ],
        compiler_params=params(16),
        cost_estimate=pl.CostEstimate(
            flops=4 * rows * chunk * heads * DV, bytes_accessed=8 << 20, transcendentals=0
        ),
        name="local",
    )(q, kt, v)


def carry(num, phi, before, prefix, chunk, first, rows):
    heads, _, count = phi.shape
    return pl.pallas_call(
        functools.partial(carry_kernel, heads),
        grid=(rows // chunk,),
        in_specs=[
            pl.BlockSpec((chunk, heads * DV), lambda i: (i + first, 0)),
            pl.BlockSpec((heads, chunk, count), lambda i: (0, i + first, 0)),
            pl.BlockSpec((1, heads, count, DV), lambda i: (i + first, 0, 0, 0)),
            pl.BlockSpec((heads, count, DV), lambda i: (0, 0, 0)),
        ],
        out_specs=pl.BlockSpec((chunk, heads * DV), lambda i: (i, 0)),
        out_shape=jax.ShapeDtypeStruct((rows, heads * DV), BF16),
        compiler_params=params(16),
        cost_estimate=pl.CostEstimate(
            flops=2 * rows * count * heads * DV, bytes_accessed=4 << 20, transcendentals=0
        ),
        name="carry",
    )(num, phi, before, prefix)


def mix_pair(order, own, other, w_out, tile):
    rows, depth = own.shape
    width = w_out.shape[1]
    grid_spec = pltpu.PrefetchScalarGridSpec(
        num_scalar_prefetch=1,
        grid=(rows // tile,),
        in_specs=[
            pl.BlockSpec((tile, depth), lambda i, o: (i, 0)),
            pl.BlockSpec((tile, depth), lambda i, o: (i, 0)),
            pl.BlockSpec((depth, width), lambda i, o: (o[0], 0)),
            pl.BlockSpec((depth, width), lambda i, o: (o[1], 0)),
        ],
        out_specs=pl.BlockSpec((tile, width), lambda i, o: (i, 0)),
    )
    return pl.pallas_call(
        mix_kernel,
        grid_spec=grid_spec,
        out_shape=jax.ShapeDtypeStruct((rows, width), BF16),
        compiler_params=params(16),
        cost_estimate=pl.CostEstimate(
            flops=4 * rows * depth * width, bytes_accessed=6 << 20, transcendentals=0
        ),
        name="mix",
    )(order, own, other, w_out, w_out)


def swap(value, axis, size, bit):
    return lax.ppermute(value, axis, [(i, i ^ bit) for i in range(size)])


def prefix_of(total, size):
    index = lax.axis_index("seq")
    if size == 1:
        return jnp.zeros_like(total)
    if size == 4:
        odd = (index % 2) == 1
        upper = index >= 2
        half = total.shape[0] // 2
        low, high = total[:half], total[half:]
        zero = jnp.zeros_like(low)
        got = swap(jnp.where(odd, low, high), "seq", size, 1)
        pair = (jnp.where(odd, high, low).astype(F32) + got.astype(F32)).astype(BF16)
        across = jnp.where(upper, swap(pair, "seq", size, 2), zero)
        send = (across.astype(F32) + jnp.where(odd, zero, low).astype(F32)).astype(BF16)
        last = swap(send, "seq", size, 1)
        first = jnp.where(odd, last, across)
        second = jnp.where(odd, got.astype(F32) + across.astype(F32), last.astype(F32)).astype(BF16)
        return jnp.concatenate([first, second], axis=0)
    prefix = jnp.zeros(total.shape, F32)
    if size & (size - 1) == 0:
        running = total.astype(F32)
        bit = 1
        while bit < size:
            got = swap(running.astype(BF16), "seq", size, bit).astype(F32)
            prefix = prefix + jnp.where((index & bit) != 0, got, jnp.zeros_like(got))
            running = running + got
            bit *= 2
        return prefix.astype(BF16)
    moved = total
    for hop in range(1, size):
        moved = lax.ppermute(moved, "seq", [(i, (i + 1) % size) for i in range(size)])
        prefix = prefix + jnp.where(index >= hop, moved.astype(F32), 0.0)
    return prefix.astype(BF16)


def local(seq_size, feat_size, tokens, w_query, w_key, value_weight, w_out):
    rows = tokens.shape[0]
    chunk = min(rows, 256)
    q, kt, v, before, total = project(tokens, w_query, w_key, value_weight, chunk)
    prefix = prefix_of(total, seq_size)
    num, phi = local_part(q, kt, v, chunk)
    if feat_size == 2:
        mine = lax.axis_index("feat").astype(jnp.int32)
        order = jnp.stack([mine, 1 - mine])
        parts = 2 if rows % (2 * chunk) == 0 else 1
        piece = rows // parts
        outs = []
        for part in range(parts):
            normed = carry(num, phi, before, prefix, chunk, part * piece // chunk, piece)
            other = swap(normed, "feat", 2, 1)
            outs.append(mix_pair(order, normed, other, w_out, chunk))
        return jnp.concatenate(outs, axis=0) if parts > 1 else outs[0]
    normed = carry(num, phi, before, prefix, chunk, 0, rows)
    full = lax.all_gather(normed, "feat", axis=1, tiled=True) if feat_size > 1 else normed
    return jnp.dot(full, w_out, preferred_element_type=F32).astype(BF16)


def solution(mesh):
    placed = (
        P(("dp", "seq"), None),
        P(None, "feat"),
        P(None, "feat"),
        P(None, "feat"),
        P(None, "feat"),
    )
    body = functools.partial(local, mesh.shape["seq"], mesh.shape["feat"])
    return jax.shard_map(
        body, mesh=mesh, in_specs=placed, out_specs=P(("dp", "seq"), "feat"), check_vma=False
    )
```

```python
import functools

import jax
import jax.numpy as jnp
from jax import lax
from jax.experimental import pallas as pl
from jax.experimental.pallas import tpu as pltpu
from jax.sharding import PartitionSpec as P

DK = 16
DV = 128
F32 = jnp.float32
BF16 = jnp.bfloat16


def feature_tiles(rows, linear, square, cross):
    half = DK // 2
    tiles = [rows * linear if linear != 1.0 else rows]
    for shift in range(half):
        other = rows if shift == 0 else pltpu.roll(rows, shift, 0)
        weight = square if shift == 0 else cross
        product = rows * other
        tiles.append(product * weight if weight != 1.0 else product)
    far = rows[:half] * rows[half:]
    one = (lax.broadcasted_iota(jnp.int32, far.shape, 0) == 0).astype(F32)
    tiles.append(jnp.concatenate([far * cross if cross != 1.0 else far, one], axis=0))
    return jnp.concatenate([tile.astype(BF16) for tile in tiles], axis=0)


def feature_count():
    return DK + (DK // 2) * DK + DK


VMEM = pl.BlockSpec(memory_space=pltpu.VMEM)
HBM = pl.BlockSpec(memory_space=pltpu.HBM)
SMEM = pl.BlockSpec(memory_space=pltpu.SMEM)


def in_hbm(value):
    return pltpu.with_memory_space_constraint(value, pltpu.HBM)


def span(index, size):
    return slice(index * size, (index + 1) * size)


def halves(count):
    middle = max(count // 2, 1)
    return range(middle), range(middle, count)


def project_kernel(
    heads, chunk, x_in, wq_in, wk_in, wv_in, q_ref, kt_ref, v_ref, before_ref, total_ref, x_ref, wq_ref, wk_ref, wv_ref, sems
):
    steps = x_in.shape[0] // chunk
    width = heads * DK
    group = 2 if heads % 2 == 0 else 1
    groups = heads // group
    cols = group * DV
    copies = {}

    def fetch(key, source, target):
        copies[key] = pltpu.make_async_copy(source, target, sems.at[len(copies)])
        copies[key].start()

    def fetch_x(m):
        rows = pl.ds(m * chunk, chunk)
        fetch(("x", m), x_in.at[rows], x_ref.at[rows])

    def wait(keys):
        for key in keys:
            copies[key].wait()

    def project_qk(m):
        rows = span(m, chunk)
        both = jnp.concatenate([wq_ref[...], wk_ref[...]], axis=1)
        qk = jnp.dot(x_ref[rows, :], both, preferred_element_type=F32)
        q_ref[rows, :] = qk[:, :width].astype(BF16)
        kt_ref[:, rows] = qk[:, width:].T.astype(BF16)

    def add_states(m, g):
        rows = span(m, chunk)
        for head in range(g * group, (g + 1) * group):
            keys = kt_ref[span(head, DK), rows].astype(F32)
            phi = feature_tiles(keys, 1.0, 1.0, 1.0)
            new = jnp.dot(phi, v_ref[rows, span(head, DV)], preferred_element_type=F32)
            if m > 0:
                new = before_ref[m - 1, head] + new
            if m < steps - 1:
                before_ref[m, head] = new
            else:
                total_ref[head] = new.astype(BF16)

    pending = []

    def project_v(m, g):
        rows = span(m, chunk)
        v_ref[rows, span(g, cols)] = jnp.dot(
            x_ref[rows, :], wv_ref[:, span(g, cols)], preferred_element_type=F32
        ).astype(BF16)
        pending.append((m, g))
        if len(pending) > 1:
            add_states(*pending.pop(0))

    early, late = halves(steps)
    fetch("q", wq_in, wq_ref)
    fetch("k", wk_in, wk_ref)
    for m in early:
        fetch_x(m)
    for g in range(groups):
        pair = pl.ds(g * cols, cols)
        fetch(("v", g), wv_in.at[:, pair], wv_ref.at[:, pair])
    for m in late:
        fetch_x(m)
    wait(["q", "k"] + [("x", m) for m in early])
    for m in early:
        project_qk(m)
    for part in halves(groups):
        wait([("v", g) for g in part])
        for m in early:
            for g in part:
                project_v(m, g)
    wait([("x", m) for m in late])
    for m in late:
        project_qk(m)
        for g in range(groups):
            project_v(m, g)
    for item in pending:
        add_states(*item)


def local_kernel(heads, chunk, q_ref, kt_ref, v_ref, w_in, num_ref, phi_ref, w_ref, sem):
    fetch = pltpu.make_async_copy(w_in, w_ref, sem)
    fetch.start()
    causal = lax.broadcasted_iota(jnp.int32, (chunk, chunk), 0) >= lax.broadcasted_iota(
        jnp.int32, (chunk, chunk), 1
    )
    owner = lax.broadcasted_iota(jnp.int32, (kt_ref.shape[0], chunk), 0) // DK
    for m in range(q_ref.shape[0] // chunk):
        rows = span(m, chunk)
        kt = kt_ref[:, rows]
        q = q_ref[rows, :].astype(F32)
        qt = q.T
        quarter = (q * 0.25).astype(BF16)
        for head in range(heads):
            keys = jnp.where(owner == head, kt, jnp.zeros_like(kt))
            s = jnp.dot(quarter, keys, preferred_element_type=F32)
            w = jnp.where(causal, 1.0 + s * (1.0 + 0.5 * s), 0.0).astype(BF16)
            cols = span(head, DV)
            num_ref[rows, cols] = jnp.dot(w, v_ref[rows, cols], preferred_element_type=F32)
            phi = feature_tiles(qt[span(head, DK)], 0.25, 1.0 / 32.0, 1.0 / 16.0)
            phi_ref[head, rows] = phi.T
    fetch.wait()


def carry_kernel(heads, chunk, first, num_ref, phi_ref, before_ref, prefix_ref, out_ref):
    for step in range(out_ref.shape[0] // chunk):
        m = first + step
        rows = span(m, chunk)
        for head in range(heads):
            cols = span(head, DV)
            state = prefix_ref[head]
            if m > 0:
                state = (state.astype(F32) + before_ref[m - 1, head]).astype(BF16)
            num = num_ref[rows, cols] + jnp.dot(phi_ref[head, rows], state, preferred_element_type=F32)
            scale = lax.rsqrt(jnp.mean(num * num, axis=-1, keepdims=True) + 1e-6)
            out_ref[span(step, chunk), cols] = (num * scale).astype(BF16)


def mix_kernel(first, tile, mine_ref, own_ref, other_ref, w_ref, *rest):
    out_ref, stage, sems = rest[-3:]
    rows, depth = own_ref.shape
    mine = mine_ref[0]
    own_rows = pl.ds(pl.multiple_of(mine * depth, depth), depth)
    other_rows = pl.ds(pl.multiple_of((1 - mine) * depth, depth), depth)
    copies = []
    for n in range(stage.shape[1] // tile):
        cols = pl.ds(n * tile, tile)
        total = jnp.dot(own_ref[...], w_ref[own_rows, cols], preferred_element_type=F32)
        total += jnp.dot(other_ref[...], w_ref[other_rows, cols], preferred_element_type=F32)
        stage[:, cols] = total.astype(BF16)
        copies.append(
            pltpu.make_async_copy(stage.at[:, cols], out_ref.at[pl.ds(first, rows), cols], sems.at[n])
        )
        copies[-1].start()
    for copy in copies:
        copy.wait()


def params(mib):
    return pltpu.CompilerParams(vmem_limit_bytes=mib << 20)


def project(x, w_query, w_key, value_weight, chunk):
    rows, depth = x.shape
    heads = value_weight.shape[1] // DV
    steps = rows // chunk
    count = feature_count()
    width = heads * DK
    return pl.pallas_call(
        functools.partial(project_kernel, heads, chunk),
        in_specs=[HBM] * 4,
        out_specs=[VMEM] * 5,
        out_shape=[
            jax.ShapeDtypeStruct((rows, width), BF16),
            jax.ShapeDtypeStruct((width, rows), BF16),
            jax.ShapeDtypeStruct((rows, heads * DV), BF16),
            jax.ShapeDtypeStruct((max(steps - 1, 1), heads, count, DV), F32),
            jax.ShapeDtypeStruct((heads, count, DV), BF16),
        ],
        scratch_shapes=[
            pltpu.VMEM((rows, depth), BF16),
            pltpu.VMEM((depth, width), BF16),
            pltpu.VMEM((depth, width), BF16),
            pltpu.VMEM((depth, heads * DV), BF16),
            pltpu.SemaphoreType.DMA((2 + steps + heads,)),
        ],
        compiler_params=params(20),
        cost_estimate=pl.CostEstimate(
            flops=2 * rows * depth * heads * (DV + 2 * DK), bytes_accessed=12 << 20, transcendentals=0
        ),
        name="project",
    )(in_hbm(x), in_hbm(w_query), in_hbm(w_key), in_hbm(value_weight))


def local_part(q, kt, v, w_out, chunk):
    rows, width = q.shape
    heads = width // DK
    count = feature_count()
    return pl.pallas_call(
        functools.partial(local_kernel, heads, chunk),
        in_specs=[VMEM] * 3 + [HBM],
        out_specs=[VMEM] * 3,
        out_shape=[
            jax.ShapeDtypeStruct((rows, heads * DV), F32),
            jax.ShapeDtypeStruct((heads, rows, count), BF16),
            jax.ShapeDtypeStruct(w_out.shape, BF16),
        ],
        scratch_shapes=[pltpu.SemaphoreType.DMA],
        compiler_params=params(4),
        cost_estimate=pl.CostEstimate(
            flops=8 * rows * chunk * heads * DV, bytes_accessed=8 << 20, transcendentals=0
        ),
        name="local",
    )(q, kt, v, in_hbm(w_out))


def carry(num, phi, before, prefix, chunk, first, rows):
    heads, _, count = phi.shape
    return pl.pallas_call(
        functools.partial(carry_kernel, heads, chunk, first),
        in_specs=[VMEM] * 4,
        out_specs=VMEM,
        out_shape=jax.ShapeDtypeStruct((rows, heads * DV), BF16),
        compiler_params=params(4),
        cost_estimate=pl.CostEstimate(
            flops=2 * rows * count * heads * DV, bytes_accessed=4 << 20, transcendentals=0
        ),
        name="carry",
    )(num, phi, before, prefix)


def mix_pair(mine, own, other, w_out, first, total_rows, earlier):
    rows, depth = own.shape
    width = w_out.shape[1]
    tile = 256 if width % 256 == 0 else width
    operands = [mine, own, other, w_out]
    specs = [SMEM, VMEM, VMEM, VMEM]
    aliases = {}
    if earlier is not None:
        operands.append(earlier)
        specs.append(HBM)
        aliases = {4: 0}
    return pl.pallas_call(
        functools.partial(mix_kernel, first, tile),
        in_specs=specs,
        out_specs=HBM,
        out_shape=jax.ShapeDtypeStruct((total_rows, width), BF16),
        scratch_shapes=[pltpu.VMEM((rows, width), BF16), pltpu.SemaphoreType.DMA((width // tile,))],
        input_output_aliases=aliases,
        compiler_params=params(6),
        cost_estimate=pl.CostEstimate(
            flops=4 * rows * depth * width, bytes_accessed=6 << 20, transcendentals=0
        ),
        name="mix",
    )(*operands)


def swap(value, axis, size, bit):
    return lax.ppermute(value, axis, [(i, i ^ bit) for i in range(size)])


def prefix_of(total, index, odd, upper, size, beside):
    if size == 1:
        return jnp.zeros_like(total), beside
    if size == 4:
        half = total.shape[0] // 2
        low, high = total[:half], total[half:]
        zero = jnp.zeros_like(low)
        got = swap(jnp.where(odd, low, high), "seq", size, 1)
        pair = (jnp.where(odd, high, low).astype(F32) + got.astype(F32)).astype(BF16)
        across = jnp.where(upper, swap(pair, "seq", size, 2), zero)
        send = (across.astype(F32) + jnp.where(odd, zero, low).astype(F32)).astype(BF16)
        send, beside = lax.optimization_barrier((send, beside))
        last = swap(send, "seq", size, 1)
        first = jnp.where(odd, last, across)
        second = jnp.where(odd, got.astype(F32) + across.astype(F32), last.astype(F32)).astype(BF16)
        return jnp.concatenate([first, second], axis=0), beside
    prefix = jnp.zeros(total.shape, F32)
    if size & (size - 1) == 0:
        running = total.astype(F32)
        bit = 1
        while bit < size:
            got = swap(running.astype(BF16), "seq", size, bit).astype(F32)
            prefix = prefix + jnp.where((index & bit) != 0, got, jnp.zeros_like(got))
            running = running + got
            bit *= 2
        return prefix.astype(BF16), beside
    moved = total
    for hop in range(1, size):
        moved = lax.ppermute(moved, "seq", [(i, (i + 1) % size) for i in range(size)])
        prefix = prefix + jnp.where(index >= hop, moved.astype(F32), 0.0)
    return prefix.astype(BF16), beside


def local(seq_size, feat_size, tokens, w_query, w_key, value_weight, w_out):
    rows = tokens.shape[0]
    chunk = 256 if rows % 256 == 0 else rows
    index = lax.axis_index("seq")
    mine = lax.axis_index("feat").astype(jnp.int32).reshape(1)
    place = (tokens, index, (index & 1) == 1, index >= 2, mine)
    tokens, index, odd, upper, mine = lax.optimization_barrier(place)
    q, kt, v, before, total = project(tokens, w_query, w_key, value_weight, chunk)
    num, phi, weight = local_part(q, kt, v, w_out, chunk)
    prefix, (num, phi, weight) = prefix_of(total, index, odd, upper, seq_size, (num, phi, weight))
    if feat_size == 2:
        parts = 2 if rows % (2 * chunk) == 0 else 1
        piece = rows // parts
        out = None
        for part in range(parts):
            normed = carry(num, phi, before, prefix, chunk, part * piece // chunk, piece)
            other = swap(normed, "feat", 2, 1)
            out = mix_pair(mine, normed, other, weight, part * piece, rows, out)
        return out
    normed = carry(num, phi, before, prefix, chunk, 0, rows)
    full = lax.all_gather(normed, "feat", axis=1, tiled=True) if feat_size > 1 else normed
    return jnp.dot(full, weight, preferred_element_type=F32).astype(BF16)


def solution(mesh):
    placed = (
        P(("dp", "seq"), None),
        P(None, "feat"),
        P(None, "feat"),
        P(None, "feat"),
        P(None, "feat"),
    )
    body = functools.partial(local, mesh.shape["seq"], mesh.shape["feat"])
    return jax.shard_map(
        body, mesh=mesh, in_specs=placed, out_specs=P(("dp", "seq"), "feat"), check_vma=False
    )
```

```python
import functools

import jax
import jax.numpy as jnp
from jax import lax
from jax.experimental import pallas as pl
from jax.experimental.pallas import tpu as pltpu
from jax.sharding import PartitionSpec as P

DK = 16
DV = 128
F32 = jnp.float32
BF16 = jnp.bfloat16


def feature_tiles(rows, linear, square, cross):
    half = DK // 2
    tiles = [rows * linear if linear != 1.0 else rows]
    for shift in range(half):
        other = rows if shift == 0 else pltpu.roll(rows, shift, 0)
        weight = square if shift == 0 else cross
        product = rows * other
        tiles.append(product * weight if weight != 1.0 else product)
    far = rows[:half] * rows[half:]
    one = (lax.broadcasted_iota(jnp.int32, far.shape, 0) == 0).astype(F32)
    tiles.append(jnp.concatenate([far * cross if cross != 1.0 else far, one], axis=0))
    return jnp.concatenate([tile.astype(BF16) for tile in tiles], axis=0)


def feature_count():
    return DK + (DK // 2) * DK + DK


VMEM = pl.BlockSpec(memory_space=pltpu.VMEM)
HBM = pl.BlockSpec(memory_space=pltpu.HBM)
SMEM = pl.BlockSpec(memory_space=pltpu.SMEM)


def in_hbm(value):
    return pltpu.with_memory_space_constraint(value, pltpu.HBM)


def span(index, size):
    return slice(index * size, (index + 1) * size)


def halves(count):
    middle = max(count // 2, 1)
    return range(middle), range(middle, count)


def project_kernel(heads, rest, chunk, *refs):
    x_in, wq_in, wk_in, wv_in, q_ref, kt_ref, v_ref, before_ref, total_ref, x_ref = refs[:10]
    later_ref = refs[10] if rest else None
    wq_ref, wk_ref, wv_ref, sems = refs[-4:]
    steps = x_in.shape[0] // chunk
    width = kt_ref.shape[0]
    group = 2 if heads % 2 == 0 else 1
    groups = heads // group
    cols = group * DV
    copies = {}

    def fetch(key, source, target):
        copies[key] = pltpu.make_async_copy(source, target, sems.at[len(copies)])
        copies[key].start()

    def fetch_x(m):
        rows = pl.ds(m * chunk, chunk)
        fetch(("x", m), x_in.at[rows], x_ref.at[rows])

    def wait(keys):
        for key in keys:
            copies[key].wait()

    def project_qk(m):
        rows = span(m, chunk)
        both = jnp.concatenate([wq_ref[...], wk_ref[...]], axis=1)
        qk = jnp.dot(x_ref[rows, :], both, preferred_element_type=F32)
        q_ref[rows, :] = qk[:, :width].astype(BF16)
        kt_ref[:, rows] = qk[:, width:].T.astype(BF16)

    project_v = ValueSteps(0, group, chunk, steps, x_ref, wv_ref, kt_ref, v_ref, before_ref, total_ref)
    early, late = halves(steps)
    fetch("q", wq_in, wq_ref)
    fetch("k", wk_in, wk_ref)
    for m in early:
        fetch_x(m)
    for g in range(groups):
        pair = pl.ds(g * cols, cols)
        fetch(("v", g), wv_in.at[:, pair], wv_ref.at[:, pair])
    for m in late:
        fetch_x(m)
    if rest:
        fetch("later", wv_in.at[:, pl.ds(heads * DV, rest * DV)], later_ref)
    wait(["q", "k"] + [("x", m) for m in early])
    for m in early:
        project_qk(m)
    wait([("v", g) for g in range(groups)])
    for m in early:
        for g in range(groups):
            project_v(m, g)
    wait([("x", m) for m in late])
    for m in late:
        project_qk(m)
        for g in range(groups):
            project_v(m, g)
    project_v.finish()
    if rest:
        wait(["later"])


class ValueSteps:
    def __init__(self, first, group, chunk, steps, x_ref, wv_ref, kt_ref, v_ref, before_ref, total_ref):
        self.first, self.group, self.chunk, self.steps = first, group, chunk, steps
        self.x_ref, self.wv_ref, self.kt_ref, self.v_ref = x_ref, wv_ref, kt_ref, v_ref
        self.before_ref, self.total_ref = before_ref, total_ref
        self.pending = []

    def __call__(self, m, g):
        rows, cols = span(m, self.chunk), span(g, self.group * DV)
        self.v_ref[rows, cols] = jnp.dot(
            self.x_ref[rows, :], self.wv_ref[:, cols], preferred_element_type=F32
        ).astype(BF16)
        self.pending.append((m, g))
        if len(self.pending) > 1:
            self.add_states(*self.pending.pop(0))

    def finish(self):
        for item in self.pending:
            self.add_states(*item)

    def add_states(self, m, g):
        rows = span(m, self.chunk)
        for head in range(g * self.group, (g + 1) * self.group):
            keys = self.kt_ref[span(self.first + head, DK), rows].astype(F32)
            phi = feature_tiles(keys, 1.0, 1.0, 1.0)
            new = jnp.dot(phi, self.v_ref[rows, span(head, DV)], preferred_element_type=F32)
            if m > 0:
                new = self.before_ref[m - 1, head] + new
            if m < self.steps - 1:
                self.before_ref[m, head] = new
            else:
                self.total_ref[head] = new.astype(BF16)


def project_later_kernel(first, heads, chunk, x_ref, wv_ref, kt_ref, w_in, v_ref, before_ref, total_ref, w_ref, sem):
    fetch = pltpu.make_async_copy(w_in, w_ref, sem)
    fetch.start()
    steps = x_ref.shape[0] // chunk
    group = 2 if heads % 2 == 0 else 1
    project_v = ValueSteps(first, group, chunk, steps, x_ref, wv_ref, kt_ref, v_ref, before_ref, total_ref)
    for m in range(steps):
        for g in range(heads // group):
            project_v(m, g)
    project_v.finish()
    fetch.wait()


def local_kernel(first, heads, chunk, q_ref, kt_ref, v_ref, num_ref, phi_ref):
    causal = lax.broadcasted_iota(jnp.int32, (chunk, chunk), 0) >= lax.broadcasted_iota(
        jnp.int32, (chunk, chunk), 1
    )
    owner = lax.broadcasted_iota(jnp.int32, (kt_ref.shape[0], chunk), 0) // DK
    for m in range(q_ref.shape[0] // chunk):
        rows = span(m, chunk)
        kt = kt_ref[:, rows]
        q = q_ref[rows, :].astype(F32)
        qt = q.T
        quarter = (q * 0.25).astype(BF16)
        for head in range(heads):
            keys = jnp.where(owner == first + head, kt, jnp.zeros_like(kt))
            s = jnp.dot(quarter, keys, preferred_element_type=F32)
            w = jnp.where(causal, 1.0 + s * (1.0 + 0.5 * s), 0.0).astype(BF16)
            cols = span(head, DV)
            num_ref[rows, cols] = jnp.dot(w, v_ref[rows, cols], preferred_element_type=F32)
            phi = feature_tiles(qt[span(first + head, DK)], 0.25, 1.0 / 32.0, 1.0 / 16.0)
            phi_ref[head, rows] = phi.T


def carry_kernel(heads, chunk, num_ref, phi_ref, before_ref, prefix_ref, out_ref):
    for m in range(out_ref.shape[0] // chunk):
        rows = span(m, chunk)
        for head in range(heads):
            cols = span(head, DV)
            state = prefix_ref[head]
            if m > 0:
                state = (state.astype(F32) + before_ref[m - 1, head]).astype(BF16)
            num = num_ref[rows, cols] + jnp.dot(phi_ref[head, rows], state, preferred_element_type=F32)
            scale = lax.rsqrt(jnp.mean(num * num, axis=-1, keepdims=True) + 1e-6)
            out_ref[rows, cols] = (num * scale).astype(BF16)


def weight_rows(mine, owner, offset, depth, w_ref):
    half = w_ref.shape[0] // 2
    start = jnp.where(owner == 0, mine, 1 - mine) * half + offset
    return pl.ds(pl.multiple_of(start, depth), depth)


def mix_kernel(offset, terms, tile, chained, final, mine_ref, w_ref, *refs):
    values, refs = refs[: len(terms)], refs[len(terms) :]
    running = refs[0] if chained else None
    out_ref = refs[1] if chained else refs[0]
    rows, depth = values[0].shape
    mine = mine_ref[0]
    copies = []
    for n in range(w_ref.shape[1] // tile):
        cols = pl.ds(n * tile, tile)
        total = running[:, cols] if chained else None
        for owner, value in zip(terms, values):
            product = jnp.dot(
                value[...], w_ref[weight_rows(mine, owner, offset, depth, w_ref), cols], preferred_element_type=F32
            )
            total = product if total is None else total + product
        if not final:
            out_ref[:, cols] = total
            continue
        stage, sems = refs[-2:]
        stage[:, cols] = total.astype(BF16)
        copies.append(pltpu.make_async_copy(stage.at[:, cols], out_ref.at[:, cols], sems.at[n]))
        copies[-1].start()
    for copy in copies:
        copy.wait()


def params(mib):
    return pltpu.CompilerParams(vmem_limit_bytes=mib << 20)


def cost(flops, mib):
    return pl.CostEstimate(flops=flops, bytes_accessed=mib << 20, transcendentals=0)


def project(x, w_query, w_key, value_weight, heads, chunk):
    rows, depth = x.shape
    rest = value_weight.shape[1] // DV - heads
    steps = rows // chunk
    count = feature_count()
    width = w_query.shape[1]
    shapes = [
        jax.ShapeDtypeStruct((rows, width), BF16),
        jax.ShapeDtypeStruct((width, rows), BF16),
        jax.ShapeDtypeStruct((rows, heads * DV), BF16),
        jax.ShapeDtypeStruct((max(steps - 1, 1), heads, count, DV), F32),
        jax.ShapeDtypeStruct((heads, count, DV), BF16),
        jax.ShapeDtypeStruct((rows, depth), BF16),
    ]
    if rest:
        shapes.append(jax.ShapeDtypeStruct((depth, rest * DV), BF16))
    return pl.pallas_call(
        functools.partial(project_kernel, heads, rest, chunk),
        in_specs=[HBM] * 4,
        out_specs=[VMEM] * len(shapes),
        out_shape=shapes,
        scratch_shapes=[
            pltpu.VMEM((depth, width), BF16),
            pltpu.VMEM((depth, width), BF16),
            pltpu.VMEM((depth, heads * DV), BF16),
            pltpu.SemaphoreType.DMA((3 + steps + heads,)),
        ],
        compiler_params=params(12),
        cost_estimate=cost(2 * rows * depth * (heads * DV + 2 * width), 12),
        name="project",
    )(in_hbm(x), in_hbm(w_query), in_hbm(w_key), in_hbm(value_weight))


def project_later(x, weight, kt, w_out, first, chunk):
    rows, depth = x.shape
    heads = weight.shape[1] // DV
    steps = rows // chunk
    count = feature_count()
    return pl.pallas_call(
        functools.partial(project_later_kernel, first, heads, chunk),
        in_specs=[VMEM] * 3 + [HBM],
        out_specs=[VMEM] * 4,
        out_shape=[
            jax.ShapeDtypeStruct((rows, heads * DV), BF16),
            jax.ShapeDtypeStruct((max(steps - 1, 1), heads, count, DV), F32),
            jax.ShapeDtypeStruct((heads, count, DV), BF16),
            jax.ShapeDtypeStruct(w_out.shape, BF16),
        ],
        scratch_shapes=[pltpu.SemaphoreType.DMA],
        compiler_params=params(4),
        cost_estimate=cost(2 * rows * depth * heads * DV, 8),
        name="project_later",
    )(x, weight, kt, in_hbm(w_out))


def local_part(q, kt, v, first, chunk):
    rows = q.shape[0]
    heads = v.shape[1] // DV
    count = feature_count()
    return pl.pallas_call(
        functools.partial(local_kernel, first, heads, chunk),
        in_specs=[VMEM] * 3,
        out_specs=[VMEM] * 2,
        out_shape=[
            jax.ShapeDtypeStruct((rows, heads * DV), F32),
            jax.ShapeDtypeStruct((heads, rows, count), BF16),
        ],
        compiler_params=params(4),
        cost_estimate=cost(8 * rows * chunk * heads * DV, 4),
        name="local",
    )(q, kt, v)


def carry(num, phi, before, prefix, chunk):
    heads, rows, count = phi.shape
    return pl.pallas_call(
        functools.partial(carry_kernel, heads, chunk),
        in_specs=[VMEM] * 4,
        out_specs=VMEM,
        out_shape=jax.ShapeDtypeStruct((rows, heads * DV), BF16),
        compiler_params=params(4),
        cost_estimate=cost(2 * rows * count * heads * DV, 4),
        name="carry",
    )(num, phi, before, prefix)


def mix(mine, w_out, terms, values, offset, running=None, final=False):
    rows, depth = values[0].shape
    width = w_out.shape[1]
    tile = 256 if width % 256 == 0 else width
    operands = [mine, w_out] + list(values) + ([] if running is None else [running])
    scratch = [pltpu.VMEM((rows, width), BF16), pltpu.SemaphoreType.DMA((width // tile,))]
    return pl.pallas_call(
        functools.partial(mix_kernel, offset, terms, tile, running is not None, final),
        in_specs=[SMEM] + [VMEM] * (len(operands) - 1),
        out_specs=HBM if final else VMEM,
        out_shape=jax.ShapeDtypeStruct((rows, width), BF16 if final else F32),
        scratch_shapes=scratch if final else [],
        compiler_params=params(8),
        cost_estimate=cost(2 * len(terms) * rows * depth * width, 4),
        name="mix",
    )(*operands)


def swap(value, axis, size, bit):
    return lax.ppermute(value, axis, [(i, i ^ bit) for i in range(size)])


def widen(value):
    return value.astype(F32)


class QuadPrefix:
    def __init__(self, total, odd, upper):
        half = total.shape[0] // 2
        self.low, self.high = total[:half], total[half:]
        self.odd, self.upper = odd, upper
        self.zero = jnp.zeros_like(self.low)

    def send_first(self):
        return jnp.where(self.odd, self.low, self.high)

    def send_second(self, first):
        self.first = first
        return (jnp.where(self.odd, widen(self.high), widen(self.low)) + widen(first)).astype(BF16)

    def send_third(self, second):
        self.across = jnp.where(self.upper, second, self.zero)
        return (widen(self.across) + jnp.where(self.odd, 0.0, widen(self.low))).astype(BF16)

    def finish(self, third):
        low = jnp.where(self.odd, third, self.across)
        high = jnp.where(self.odd, widen(self.first) + widen(self.across), widen(third)).astype(BF16)
        return jnp.concatenate([low, high], axis=0)


def any_prefix(total, index, size):
    if size == 1:
        return jnp.zeros_like(total)
    prefix = jnp.zeros(total.shape, F32)
    if size & (size - 1) == 0:
        running = widen(total)
        bit = 1
        while bit < size:
            got = widen(swap(running.astype(BF16), "seq", size, bit))
            prefix = prefix + jnp.where((index & bit) != 0, got, 0.0)
            running = running + got
            bit *= 2
        return prefix.astype(BF16)
    moved = total
    for hop in range(1, size):
        moved = lax.ppermute(moved, "seq", [(i, (i + 1) % size) for i in range(size)])
        prefix = prefix + jnp.where(index >= hop, widen(moved), 0.0)
    return prefix.astype(BF16)


def local(seq_size, feat_size, tokens, w_query, w_key, value_weight, w_out):
    rows = tokens.shape[0]
    heads = value_weight.shape[1] // DV
    chunk = 256 if rows % 256 == 0 else rows
    index = lax.axis_index("seq")
    mine = lax.axis_index("feat").astype(jnp.int32).reshape(1)
    place = (tokens, index, (index & 1) == 1, index >= 2, mine)
    tokens, index, odd, upper, mine = lax.optimization_barrier(place)
    if seq_size != 4 or feat_size != 2 or heads % 4 != 0:
        q, kt, v, before, total, _ = project(tokens, w_query, w_key, value_weight, heads, chunk)
        prefix = any_prefix(total, index, seq_size)
        num, phi = local_part(q, kt, v, 0, chunk)
        normed = carry(num, phi, before, prefix, chunk)
        full = lax.all_gather(normed, "feat", axis=1, tiled=True) if feat_size > 1 else normed
        return jnp.dot(full, w_out, preferred_element_type=F32).astype(BF16)

    together = lax.optimization_barrier
    near = functools.partial(swap, axis="seq", size=4, bit=1)
    far = functools.partial(swap, axis="seq", size=4, bit=2)
    twin = functools.partial(swap, axis="feat", size=2, bit=1)
    part = heads // 2
    q, kt, v_a, before_a, total_a, x, later = project(tokens, w_query, w_key, value_weight, part, chunk)
    prefix_a = QuadPrefix(total_a, odd, upper)
    a1 = near(prefix_a.send_first())
    v_b, before_b, total_b, weight = project_later(x, later, kt, w_out, part, chunk)
    prefix_b = QuadPrefix(total_b, odd, upper)
    send_a, send_b, q = together((prefix_a.send_second(a1), prefix_b.send_first(), q))
    a2 = far(send_a)
    b1 = near(send_b)
    num_a, phi_a = local_part(q, kt, v_a, 0, chunk)
    send_b, num_a, phi_a, q = together((prefix_b.send_second(b1), num_a, phi_a, q))
    b2 = far(send_b)
    a3 = near(prefix_a.send_third(a2))
    num_b, phi_b = local_part(q, kt, v_b, part, chunk)
    sum_a, num_b, phi_b = together((prefix_a.finish(a3), num_b, phi_b))
    normed_a = carry(num_a, phi_a, before_a, sum_a, chunk)
    other_a = twin(normed_a)
    send_b, other_a = together((prefix_b.send_third(b2), other_a))
    b3 = near(send_b)
    running = mix(mine, weight, (0, 1), (normed_a, other_a), 0)
    sum_b, running = together((prefix_b.finish(b3), running))
    normed_b = carry(num_b, phi_b, before_b, sum_b, chunk)
    other_b = twin(normed_b)
    running = mix(mine, weight, (0,), (normed_b,), part * DV, running)
    return mix(mine, weight, (1,), (other_b,), part * DV, running, final=True)


def solution(mesh):
    placed = (
        P(("dp", "seq"), None),
        P(None, "feat"),
        P(None, "feat"),
        P(None, "feat"),
        P(None, "feat"),
    )
    body = functools.partial(local, mesh.shape["seq"], mesh.shape["feat"])
    return jax.shard_map(
        body, mesh=mesh, in_specs=placed, out_specs=P(("dp", "seq"), "feat"), check_vma=False
    )
```
